32 devices in a mesh: elem: 16 (over z, x, core), band: 2 (over y).
Axes of the slice: x: 2, y: 2, z: 4, core: 2. Of those that a mesh axis runs over, the one named last changes fastest.
Arguments:
- basis: bfloat16 [256, 32, 16, 160], P('band', 'elem'), may hold values from -8 to 8
- hamiltonian: bfloat16 [32, 16, 7, 160, 160], P('elem'), may hold values from -0.09375 to 0.09375
- neighbours: int32 [32, 16, 6], P('elem'), may hold values from 0 to 511, as said below
Outputs:
- filtered: bfloat16 [256, 32, 16, 160], P('band', 'elem')
- intersection: float32 [256, 256], P('elem', 'band')
- projected: float32 [256, 256], P('elem', 'band')
The draws below stay inside these ranges and needn't reach their ends.
Inputs may be any that keep to these rules, and one draw needn't show every extreme that they name: neighbours[z, s, d] = z2 * 16 + s2 names the element (z2, s2) that shares face d with element (z, s) on a periodic grid of 4 x 4 x 32 cells, whose cells are stored within each layer in an order of the draw; faces 0 to 3 lie in the same layer z, face 4 in layer z - 1 and face 5 in layer z + 1, both modulo 32.
All inputs are finite; a program needn't handle non-finite values.
Results may differ from the reference program's by a relative error of at most 0.0075.
Values may be sent and summed in bfloat16 or wider, within the bound.
A program may use at most 64 MiB of HBM per device.

```python
import jax
import jax.numpy as jnp

NB = 160
BANDS = 256
CX = 4
CY = 4
DEGREE = 4
CXY = 16
NZ = 32


def draw_neighbours(key, part):
    layer_keys = jax.random.split(jax.random.fold_in(key, 17), NZ)
    cells = CX * CY
    orders = jax.vmap(lambda k: jax.random.permutation(k, cells))(layer_keys).astype(jnp.int32)
    places = jnp.argsort(orders, axis=1).astype(jnp.int32)
    across = orders // CY
    along = orders % CY
    minus_x = (across - 1) % CX * CY + along
    plus_x = (across + 1) % CX * CY + along
    minus_y = across * CY + (along - 1) % CY
    plus_y = across * CY + (along + 1) % CY
    layers = jnp.arange(NZ).astype(jnp.int32)[:, None] * jnp.ones((1, cells), jnp.int32)
    same = [jnp.take_along_axis(places, target, axis=1) + layers * cells for target in (minus_x, plus_x, minus_y, plus_y)]
    below = jnp.roll(places, 1, axis=0)
    above = jnp.roll(places, -1, axis=0)
    lower = jnp.take_along_axis(below, orders, axis=1) + (layers - 1) % NZ * cells
    upper = jnp.take_along_axis(above, orders, axis=1) + (layers + 1) % NZ * cells
    return jnp.stack(same + [lower, upper], axis=-1).astype(jnp.int32)


def draw_basis(key, part):
    base = jax.random.fold_in(key, 29)
    key_noise, key_common, key_group, key_weight = jax.random.split(base, 4)
    families = 16
    shape = (BANDS, NZ, CX * CY, NB)
    groups = jax.random.randint(key_group, (BANDS,), 0, families).astype(jnp.int32)
    noise = jax.random.normal(key_noise, shape, jnp.float32)
    common = jax.random.normal(key_common, (families, NZ, CX * CY, NB), jnp.float32)
    weight = jax.random.normal(key_weight, (BANDS, 1, 1, 1), jnp.float32)
    shared = jnp.take(common, groups, axis=0)
    value = noise + weight * shared
    return jnp.clip(value, -8.0, 8.0).astype(jnp.bfloat16)


def block_levels(stream_key, extent, cuts, low, largest):
    def one(dim, shards_of):
        heights = jax.random.uniform(jax.random.fold_in(jax.random.fold_in(stream_key, 6), dim), (shards_of,), jnp.float32, low / len(cuts), largest / len(cuts))
        return jnp.repeat(jnp.exp(heights), extent[dim] // shards_of).reshape((-1,) + (1,) * (len(extent) - dim - 1))

    level = one(*cuts[0])
    for cut in cuts[1:]:
        level = level * one(*cut)
    return level


def centred(rng, shape, spread, reach, shards=(), dtype=jnp.bfloat16):
    loudness = block_levels(rng, shape, shards, -0.22, 0.18) if shards else 1.0
    array = jax.random.normal(rng, shape, jnp.float32) * spread * loudness
    return jnp.minimum(jnp.maximum(array, -reach), reach).astype(dtype)


def setup_inputs(seed: int = 0) -> dict:
    seeds = jax.random.split(jax.random.key(seed), 4)
    basis = draw_basis(jax.random.fold_in(seeds[3], 71), 0)
    hamiltonian = centred(seeds[1], (NZ, CXY, 7, NB, NB), (28 * NB) ** -0.5, 0.09375, ((0, 16),))
    neighbours = draw_neighbours(jax.random.fold_in(seeds[3], 71), 0)
    return dict(basis=basis, hamiltonian=hamiltonian, neighbours=neighbours)


def apply_blocks(flat, blocks, table):
    total = jnp.zeros(flat.shape, jnp.float32)
    for face in range(7):
        picked = jnp.take(flat, table[:, face], axis=1).astype(jnp.float32)
        total = total + jnp.einsum("eij,bej->bei", blocks[:, face].astype(jnp.float32), picked)
    return total


def reference(basis, hamiltonian, neighbours):
    count = NZ * CX * CY
    flat = basis.reshape(BANDS, count, NB)
    blocks = hamiltonian.reshape(count, 7, NB, NB)
    own = jnp.arange(count).astype(jnp.int32)[:, None]
    table = jnp.concatenate([own, neighbours.reshape(count, 6).astype(jnp.int32)], axis=1)
    previous = flat
    current = apply_blocks(flat, blocks, table).astype(jnp.bfloat16)
    for step in range(DEGREE - 1):
        following = (2.0 * apply_blocks(current, blocks, table) - previous.astype(jnp.float32)).astype(jnp.bfloat16)
        previous, current = current, following
    image = apply_blocks(current, blocks, table).astype(jnp.bfloat16)
    factor = 1.0 / (count * NB)
    left = current.astype(jnp.float32)
    intersection = jnp.einsum("aei,bei->ab", left, left) * factor
    projected = jnp.einsum("aei,bei->ab", left, image.astype(jnp.float32)) * factor
    return current.reshape(BANDS, NZ, CX * CY, NB), intersection, projected
```

```python
import functools

import jax
import jax.numpy as jnp
from jax import lax
from jax.experimental import pallas as pl
from jax.experimental.pallas import tpu as pltpu
from jax.sharding import PartitionSpec as P

DEGREE = 4
PIECES = 4
MESH = pl.DeviceIdType.MESH
F32 = jnp.float32
BF16 = jnp.bfloat16


def dot(a, b):
    return jnp.dot(a, b, preferred_element_type=F32)


def kernel(
    geom,
    nbr,
    y0_hbm,
    ham_hbm,
    f_out,
    s_out,
    p_out,
    ham,
    y0,
    buf_a,
    buf_b,
    near0,
    near1,
    far0,
    far1,
    stage0,
    stage1,
    ordered,
    fi,
    sums,
    others,
    parts,
    got1,
    mid,
    got2,
    tab,
    ham_sem,
    y0_sem,
    out_sem,
    near_send,
    near_recv,
    far_send,
    far_recv,
    fsend,
    frecv,
    r1send,
    r1recv,
    r2send,
    r2recv,
):
    n, nband, cells, n1, n2, rows, factor = geom
    total = 2 * cells
    bands = y0.shape[2]
    me = lax.axis_index("elem")
    bme = lax.axis_index("band")
    right, left = lax.rem(me + 1, n), lax.rem(me + n - 1, n)
    group, member = me // n1, me % n1

    first = pltpu.make_async_copy(y0_hbm, y0, y0_sem)
    first.start()
    hcopies = []
    hparts = ham_sem.shape[0]
    for c in range(hparts):
        size = ham.shape[0] // hparts
        window = pl.ds(c * size, size)
        hc = pltpu.make_async_copy(ham_hbm.at[window], ham.at[window], ham_sem.at[c])
        hc.start()
        hcopies.append(hc)

    barrier = pltpu.get_barrier_semaphore()
    peers = [{"elem": left}, {"elem": right}]
    for j in range(1, nband):
        peers.append({"band": lax.rem(bme + j, nband)})
    for j in range(1, n1):
        peers.append({"elem": group * n1 + lax.rem(member + j, n1)})
    for j in range(1, n2):
        peers.append({"elem": lax.rem(group + j, n2) * n1 + member})
    for peer in peers:
        pl.semaphore_signal(barrier, inc=1, device_id=peer, device_id_type=MESH)

    core = me % 2
    near_base, far_base = (1 - core) * cells, core * cells
    near_peer = me + 1 - 2 * core
    far_peer = lax.rem(me + n - 1 + 2 * core, n)
    nears, fars, stages = (near0, near1), (far0, far1), (stage0, stage1)
    piece = cells // PIECES

    down = [lax.rem(nbr[4, 0, c], cells) for c in range(cells)]
    for c in range(cells):
        tab[6, far_base + c] = far_base + jnp.where(core == 0, down[c], c)

    def far_slots(i, carry):
        cell = jnp.int32(0)
        for c in range(cells):
            cell = jnp.where(down[c] == i, c, cell)
        cell = jnp.where(core == 0, cell, i)
        tab[0, far_base + i] = far_base + cell
        return carry

    lax.fori_loop(0, cells, far_slots, 0)

    def near_slots(i, carry):
        above = lax.rem(nbr[4 + core, 1 - core, i], cells)
        tab[6, near_base + i] = tab[6, far_base + above] - far_base + near_base
        cell = lax.rem(nbr[5 - core, core, tab[0, far_base + i] - far_base], cells)
        tab[0, near_base + i] = near_base + cell
        tab[5, near_base + i] = lax.rem(nbr[5 - core, 1 - core, cell], cells)
        return carry

    lax.fori_loop(0, cells, near_slots, 0)
    first.wait()

    def order(i, carry):
        buf_b[far_base + i] = y0[tab[0, far_base + i]]
        return carry

    lax.fori_loop(0, cells, order, 0, unroll=4)
    pl.semaphore_wait(barrier, len(peers))

    def near_copy(step):
        source = y0.at[pl.ds(near_base, cells)] if step == 0 else stages[step % 2]
        return pltpu.make_async_remote_copy(
            src_ref=source,
            dst_ref=nears[step % 2],
            send_sem=near_send.at[step],
            recv_sem=near_recv.at[step],
            device_id={"elem": near_peer},
            device_id_type=MESH,
        )

    def far_copy(step, p):
        source = buf_b if step % 2 == 0 else buf_a
        return pltpu.make_async_remote_copy(
            src_ref=source.at[pl.ds(far_base + p * piece, piece)],
            dst_ref=fars[step % 2].at[pl.ds(p * piece, piece)],
            send_sem=far_send.at[step, p],
            recv_sem=far_recv.at[step, p],
            device_id={"elem": far_peer},
            device_id_type=MESH,
        )

    def field_copy(j, layer, p):
        base = near_base if layer == 0 else far_base
        return pltpu.make_async_remote_copy(
            src_ref=buf_b.at[pl.ds(base + p * piece, piece)],
            dst_ref=others.at[j - 1, layer, pl.ds(p * piece, piece)],
            send_sem=fsend.at[j - 1, layer, p],
            recv_sem=frecv.at[j - 1, layer, p],
            device_id={"band": lax.rem(bme + j, nband)},
            device_id_type=MESH,
        )

    for p in range(PIECES):
        far_copy(0, p).start()
    near_copy(0).start()

    def order_near(i, carry):
        buf_b[near_base + i] = y0[tab[0, near_base + i]]
        return carry

    lax.fori_loop(0, cells, order_near, 0, unroll=4)

    def layer_slots(i, carry):
        for layer in range(2):
            own = layer * cells
            cell = tab[0, own + i] - own
            for d in range(4):
                other = lax.rem(nbr[d, layer, cell], cells)
                tab[1 + d, own + i] = tab[6, own + other]
        return carry

    lax.fori_loop(0, cells, layer_slots, 0)
    for t in range(nband):
        sums[t] = jnp.zeros(sums.shape[1:], F32)
    for hc in hcopies:
        hc.wait()

    def gram(t, slot, field):
        sums[t] += sum(dot(fi[slot + i], field(i)) for i in range(piece))

    def gram_own(base, p):
        gram(0, base + p * piece, lambda i: buf_b[base + p * piece + i])

    def gram_other(j, layer, p):
        base = near_base if layer == 0 else far_base
        field_copy(j, layer, p).wait_recv()
        gram(j, base + p * piece, lambda i: others[j - 1, layer, p * piece + i])

    written = pltpu.make_async_copy(ordered, f_out, out_sem)
    for step in range(DEGREE + 1):
        last = step == DEGREE
        current, target = (buf_b, buf_a) if step % 2 == 0 else (buf_a, buf_b)
        near_halo, far_halo = nears[step % 2], fars[step % 2]

        def cell(base, i, straight, halo, step=step, current=current, target=target):
            slot = base + i
            block = tab[0, slot] * 7
            value = dot(ham[block], current[slot])
            for d in range(4):
                value += dot(ham[block + d + 1], current[tab[1 + d, slot]])
            value += dot(ham[block + straight], current[near_base + far_base - base + i])
            value += dot(ham[block + 11 - straight], halo)
            if step > 0 and step < DEGREE:
                value = 2.0 * value - target[slot].astype(F32)
            if step < DEGREE:
                target[slot] = value.astype(BF16)
            if step == DEGREE - 1:
                fi[slot, :bands] = value.T.astype(BF16)
            if step == DEGREE:
                fi[slot, bands:] = value.T.astype(BF16)

        near_copy(step).wait_recv()

        def do(
            p,
            carry,
            step=step,
            last=last,
            target=target,
            near_halo=near_halo,
            far_halo=far_halo,
            cell=cell,
        ):
            for t in range(piece):
                i = p * piece + t
                cell(near_base, i, 5 + core, near_halo[tab[5, near_base + i]])
            if step == DEGREE - 1:
                for j in range(1, nband):
                    field_copy(j, 0, p).start()
            if not last:

                @pl.when(p == PIECES - 1)
                def _():
                    if step > 0:
                        near_copy(step - 1).wait_send()

                    def put_near(i, carry):
                        stages[(step + 1) % 2][i] = target[tab[6, near_base + i]]
                        return carry

                    lax.fori_loop(0, cells, put_near, 0, unroll=4)
                    near_copy(step + 1).start()

            else:
                share = total // PIECES

                def put_out(i, carry):
                    ordered[p * share + i] = buf_b[tab[6, p * share + i]]
                    return carry

                lax.fori_loop(0, share, put_out, 0, unroll=4)
                gram_own(near_base, p)

                @pl.when(p > 0)
                def _():
                    for j in range(1, nband):
                        for layer in range(2):
                            gram_other(j, layer, p - 1)

            far_copy(step, p).wait_recv()
            if step > 0:
                far_copy(step - 1, p).wait_send()
            for t in range(piece):
                i = p * piece + t
                cell(far_base, i, 6 - core, far_halo[i])
            if not last:
                far_copy(step + 1, p).start()
            if step == DEGREE - 1:
                for j in range(1, nband):
                    field_copy(j, 1, p).start()
            if last:
                gram_own(far_base, p)
            return carry

        lax.fori_loop(0, PIECES, do, 0)
    written.start()
    near_copy(DEGREE - 1).wait_send()
    near_copy(DEGREE).wait_send()
    for p in range(PIECES):
        far_copy(DEGREE, p).wait_send()
    for j in range(1, nband):
        for layer in range(2):
            gram_other(j, layer, PIECES - 1)

    per = bands // rows

    def put(who, t):
        for u in range(2):
            block = sums[t, u * bands : (u + 1) * bands].T.reshape(per, rows, bands)
            for i in range(per):
                r = who * per + i
                parts[r % n1, r // n1, u] = block[i]

    put(bme, 0)
    for j in range(1, nband):
        put(lax.rem(bme + nband - j, nband), j)

    copies = []
    for j in range(1, n1):
        to = lax.rem(member + j, n1)
        copy = pltpu.make_async_remote_copy(
            src_ref=parts.at[to],
            dst_ref=got1.at[j - 1],
            send_sem=r1send.at[j - 1],
            recv_sem=r1recv.at[j - 1],
            device_id={"elem": group * n1 + to},
            device_id_type=MESH,
        )
        copy.start()
        copies.append(copy)
    for j in range(1, nband):
        for layer in range(2):
            for p in range(PIECES):
                field_copy(j, layer, p).wait_send()
    running = parts[member]
    for j, copy in enumerate(copies):
        copy.wait_recv()
        running += got1[j]
    mid[...] = running
    copies2 = []
    for j in range(1, n2):
        to = lax.rem(group + j, n2)
        copy = pltpu.make_async_remote_copy(
            src_ref=mid.at[to],
            dst_ref=got2.at[j - 1],
            send_sem=r2send.at[j - 1],
            recv_sem=r2recv.at[j - 1],
            device_id={"elem": to * n1 + member},
            device_id_type=MESH,
        )
        copy.start()
        copies2.append(copy)
    for copy in copies:
        copy.wait_send()
    final = mid[group]
    for j, copy in enumerate(copies2):
        copy.wait_recv()
        final += got2[j]
    for copy in copies2:
        copy.wait_send()
    written.wait()
    s_out[...] = final[0] * factor
    p_out[...] = final[1] * factor


def body(n, nband, basis, hamiltonian, neighbours):
    bands, layers, cells, funcs = basis.shape
    total = layers * cells
    depth = layers * n
    rows = bands * nband // n
    n1 = 4
    n2 = n // n1
    nbr = neighbours.transpose(2, 0, 1)
    y0 = basis.reshape(bands, total, funcs).transpose(1, 2, 0)
    ham = hamiltonian.reshape(total * 7, funcs, funcs)
    factor = 1.0 / (depth * cells * funcs)
    geom = (n, nband, cells, n1, n2, rows, factor)
    vm = pl.BlockSpec(memory_space=pltpu.VMEM)
    half = (cells, funcs, bands)
    dma = pltpu.SemaphoreType.DMA
    small = jax.ShapeDtypeStruct((rows, bands), F32)
    field, s, p = pl.pallas_call(
        functools.partial(kernel, geom),
        out_shape=(jax.ShapeDtypeStruct((total, funcs, bands), BF16), small, small),
        in_specs=[
            pl.BlockSpec(memory_space=pltpu.SMEM),
            pl.BlockSpec(memory_space=pl.ANY),
            pl.BlockSpec(memory_space=pl.ANY),
        ],
        out_specs=(pl.BlockSpec(memory_space=pl.ANY), vm, vm),
        scratch_shapes=[
            pltpu.VMEM((total * 7, funcs, funcs), BF16),
            pltpu.VMEM((total, funcs, bands), BF16),
            pltpu.VMEM((total, funcs, bands), BF16),
            pltpu.VMEM((total, funcs, bands), BF16),
            pltpu.VMEM(half, BF16),
            pltpu.VMEM(half, BF16),
            pltpu.VMEM(half, BF16),
            pltpu.VMEM(half, BF16),
            pltpu.VMEM(half, BF16),
            pltpu.VMEM(half, BF16),
            pltpu.VMEM((total, funcs, bands), BF16),
            pltpu.VMEM((total, 2 * bands, funcs), BF16),
            pltpu.VMEM((nband, 2 * bands, bands), F32),
            pltpu.VMEM((nband - 1, 2, cells, funcs, bands), BF16),
            pltpu.VMEM((n1, n2, 2, rows, bands), F32),
            pltpu.VMEM((n1 - 1, n2, 2, rows, bands), F32),
            pltpu.VMEM((n2, 2, rows, bands), F32),
            pltpu.VMEM((n2 - 1, 2, rows, bands), F32),
            pltpu.SMEM((7, total), jnp.int32),
            dma((4,)),
            dma,
            dma,
            dma((DEGREE + 1,)),
            dma((DEGREE + 1,)),
            dma((DEGREE + 1, PIECES)),
            dma((DEGREE + 1, PIECES)),
            dma((nband - 1, 2, PIECES)),
            dma((nband - 1, 2, PIECES)),
            dma((n1 - 1,)),
            dma((n1 - 1,)),
            dma((n2 - 1,)),
            dma((n2 - 1,)),
        ],
        compiler_params=pltpu.CompilerParams(
            collective_id=0, has_side_effects=True, vmem_limit_bytes=56 * 1024 * 1024
        ),
    )(nbr, y0, ham)
    filtered = field.transpose(2, 0, 1).reshape(bands, layers, cells, funcs)
    return filtered, s, p


def solution(mesh):
    placed = (
        P("band", "elem", None, None),
        P("elem", None, None, None, None),
        P("elem", None, None),
    )
    return jax.shard_map(
        functools.partial(body, mesh.shape["elem"], mesh.shape["band"]),
        mesh=mesh,
        in_specs=placed,
        out_specs=(P("band", "elem", None, None), P("elem", "band"), P("elem", "band")),
        check_vma=False,
    )
```

```python
import functools

import jax
import jax.numpy as jnp
from jax import lax
from jax.experimental import pallas as pl
from jax.experimental.pallas import tpu as pltpu
from jax.sharding import PartitionSpec as P

DEGREE = 4
PIECES = 4
MESH = pl.DeviceIdType.MESH
F32 = jnp.float32
BF16 = jnp.bfloat16


def dot(a, b):
    return jnp.dot(a, b, preferred_element_type=F32)


def kernel(
    geom,
    nbr,
    y0_hbm,
    ham_hbm,
    f_out,
    s_out,
    p_out,
    ham,
    y0,
    buf_a,
    buf_b,
    near0,
    near1,
    far0,
    far1,
    stage0,
    stage1,
    ordered,
    acc,
    fi,
    sums,
    others,
    parts,
    got1,
    mid,
    got2,
    tab,
    ham_sem,
    y0_sem,
    out_sem,
    near_send,
    near_recv,
    far_send,
    far_recv,
    fsend,
    frecv,
    r1send,
    r1recv,
    r2send,
    r2recv,
):
    n, nband, cells, n1, n2, rows, factor = geom
    total = 2 * cells
    bands = y0.shape[2]
    me = lax.axis_index("elem")
    bme = lax.axis_index("band")
    right, left = lax.rem(me + 1, n), lax.rem(me + n - 1, n)
    group, member = me // n1, me % n1

    first = pltpu.make_async_copy(y0_hbm, y0, y0_sem)
    first.start()
    hcopies = []
    hparts = ham_sem.shape[0]
    for c in range(hparts):
        size = ham.shape[0] // hparts
        window = pl.ds(c * size, size)
        hc = pltpu.make_async_copy(ham_hbm.at[window], ham.at[window], ham_sem.at[c])
        hc.start()
        hcopies.append(hc)

    barrier = pltpu.get_barrier_semaphore()
    peers = [{"elem": left}, {"elem": right}]
    for j in range(1, nband):
        peers.append({"band": lax.rem(bme + j, nband)})
    for j in range(1, n1):
        peers.append({"elem": group * n1 + lax.rem(member + j, n1)})
    for j in range(1, n2):
        peers.append({"elem": lax.rem(group + j, n2) * n1 + member})
    for peer in peers:
        pl.semaphore_signal(barrier, inc=1, device_id=peer, device_id_type=MESH)

    core = me % 2
    near_base, far_base = (1 - core) * cells, core * cells
    near_peer = me + 1 - 2 * core
    far_peer = lax.rem(me + n - 1 + 2 * core, n)
    nears, fars, stages = (near0, near1), (far0, far1), (stage0, stage1)
    piece = cells // PIECES

    down = [lax.rem(nbr[4, 0, c], cells) for c in range(cells)]
    for c in range(cells):
        tab[6, far_base + c] = far_base + jnp.where(core == 0, down[c], c)

    def far_slots(i, carry):
        cell = jnp.int32(0)
        for c in range(cells):
            cell = jnp.where(down[c] == i, c, cell)
        cell = jnp.where(core == 0, cell, i)
        tab[0, far_base + i] = far_base + cell
        return carry

    lax.fori_loop(0, cells, far_slots, 0)

    def near_slots(i, carry):
        above = lax.rem(nbr[4 + core, 1 - core, i], cells)
        tab[6, near_base + i] = tab[6, far_base + above] - far_base + near_base
        cell = lax.rem(nbr[5 - core, core, tab[0, far_base + i] - far_base], cells)
        tab[0, near_base + i] = near_base + cell
        tab[5, near_base + i] = lax.rem(nbr[5 - core, 1 - core, cell], cells)
        return carry

    lax.fori_loop(0, cells, near_slots, 0)
    first.wait()

    def order(i, carry):
        buf_b[far_base + i] = y0[tab[0, far_base + i]]
        return carry

    lax.fori_loop(0, cells, order, 0, unroll=4)
    pl.semaphore_wait(barrier, len(peers))

    def near_copy(step):
        source = y0.at[pl.ds(near_base, cells)] if step == 0 else stages[step % 2]
        return pltpu.make_async_remote_copy(
            src_ref=source,
            dst_ref=nears[step % 2],
            send_sem=near_send.at[step],
            recv_sem=near_recv.at[step],
            device_id={"elem": near_peer},
            device_id_type=MESH,
        )

    def far_copy(step, p):
        source = buf_b if step % 2 == 0 else buf_a
        return pltpu.make_async_remote_copy(
            src_ref=source.at[pl.ds(far_base + p * piece, piece)],
            dst_ref=fars[step % 2].at[pl.ds(p * piece, piece)],
            send_sem=far_send.at[step, p],
            recv_sem=far_recv.at[step, p],
            device_id={"elem": far_peer},
            device_id_type=MESH,
        )

    def field_copy(j, layer, p):
        base = near_base if layer == 0 else far_base
        return pltpu.make_async_remote_copy(
            src_ref=buf_b.at[pl.ds(base + p * piece, piece)],
            dst_ref=others.at[j - 1, layer, pl.ds(p * piece, piece)],
            send_sem=fsend.at[j - 1, layer, p],
            recv_sem=frecv.at[j - 1, layer, p],
            device_id={"band": lax.rem(bme + j, nband)},
            device_id_type=MESH,
        )

    for p in range(PIECES):
        far_copy(0, p).start()
    near_copy(0).start()

    def order_near(i, carry):
        buf_b[near_base + i] = y0[tab[0, near_base + i]]
        return carry

    lax.fori_loop(0, cells, order_near, 0, unroll=4)

    def layer_slots(i, carry):
        for layer in range(2):
            own = layer * cells
            cell = tab[0, own + i] - own
            for d in range(4):
                other = lax.rem(nbr[d, layer, cell], cells)
                tab[1 + d, own + i] = tab[6, own + other]
        return carry

    lax.fori_loop(0, cells, layer_slots, 0)
    for t in range(nband):
        sums[t] = jnp.zeros(sums.shape[1:], F32)
    for hc in hcopies:
        hc.wait()

    def gram(t, slot, field):
        sums[t] += sum(dot(fi[slot + i], field(i)) for i in range(piece))

    def gram_own(base, p):
        gram(0, base + p * piece, lambda i: buf_b[base + p * piece + i])

    def gram_other(j, layer, p):
        base = near_base if layer == 0 else far_base
        field_copy(j, layer, p).wait_recv()
        gram(j, base + p * piece, lambda i: others[j - 1, layer, p * piece + i])

    written = pltpu.make_async_copy(ordered, f_out, out_sem)
    for step in range(DEGREE + 1):
        last = step == DEGREE
        current, target = (buf_b, buf_a) if step % 2 == 0 else (buf_a, buf_b)
        near_halo, far_halo = nears[step % 2], fars[step % 2]

        def local(base, i, straight, current=current):
            slot = base + i
            block = tab[0, slot] * 7
            value = dot(ham[block], current[slot])
            for d in range(4):
                value += dot(ham[block + d + 1], current[tab[1 + d, slot]])
            across = near_base + far_base - base + i
            return value + dot(ham[block + straight], current[across])

        def finish(base, i, face, value, halo, step=step, target=target):
            slot = base + i
            value += dot(ham[tab[0, slot] * 7 + face], halo)
            if step > 0 and step < DEGREE:
                value = 2.0 * value - target[slot].astype(F32)
            if step < DEGREE:
                target[slot] = value.astype(BF16)
            if step == DEGREE - 1:
                fi[slot, :bands] = value.T.astype(BF16)
            if step == DEGREE:
                fi[slot, bands:] = value.T.astype(BF16)

        def near_piece(
            p, step=step, near_halo=near_halo, local=local, finish=finish, last=last
        ):
            for t in range(piece):
                i = p * piece + t
                halo = near_halo[tab[5, near_base + i]]
                finish(near_base, i, 6 - core, local(near_base, i, 5 + core), halo)
            if step == DEGREE - 1:
                for j in range(1, nband):
                    field_copy(j, 0, p).start()
            if last:
                gram_own(near_base, p)

        def do(
            p,
            carry,
            step=step,
            last=last,
            target=target,
            far_halo=far_halo,
            local=local,
            finish=finish,
            near_piece=near_piece,
        ):
            for t in range(piece):
                acc[t] = local(far_base, p * piece + t, 6 - core)

            @pl.when(p > 0)
            def _():
                near_piece(p)
                if last:
                    for j in range(1, nband):
                        for layer in range(2):
                            gram_other(j, layer, p - 1)

            if not last:

                @pl.when(p == PIECES - 1)
                def _():
                    if step > 0:
                        near_copy(step - 1).wait_send()

                    def put_near(i, carry):
                        stages[(step + 1) % 2][i] = target[tab[6, near_base + i]]
                        return carry

                    lax.fori_loop(0, cells, put_near, 0, unroll=4)
                    near_copy(step + 1).start()

            far_copy(step, p).wait_recv()
            if step > 0:
                far_copy(step - 1, p).wait_send()
            for t in range(piece):
                i = p * piece + t
                finish(far_base, i, 5 + core, acc[t], far_halo[i])
            if not last:
                far_copy(step + 1, p).start()
            if step == DEGREE - 1:
                for j in range(1, nband):
                    field_copy(j, 1, p).start()
            if last:
                gram_own(far_base, p)

            @pl.when(p == 0)
            def _():
                near_copy(step).wait_recv()
                near_piece(p)
                if last:

                    def put_out(e, carry):
                        ordered[e] = buf_b[tab[6, e]]
                        return carry

                    lax.fori_loop(0, total, put_out, 0, unroll=4)
                    written.start()

            return carry

        lax.fori_loop(0, PIECES, do, 0)
    near_copy(DEGREE - 1).wait_send()
    near_copy(DEGREE).wait_send()
    for p in range(PIECES):
        far_copy(DEGREE, p).wait_send()
    for j in range(1, nband):
        for layer in range(2):
            gram_other(j, layer, PIECES - 1)

    per = bands // rows

    def put(who, t):
        for u in range(2):
            block = sums[t, u * bands : (u + 1) * bands].T.reshape(per, rows, bands)
            for i in range(per):
                r = who * per + i
                parts[r % n1, r // n1, u] = block[i]

    put(bme, 0)
    for j in range(1, nband):
        put(lax.rem(bme + nband - j, nband), j)

    copies = []
    for j in range(1, n1):
        to = lax.rem(member + j, n1)
        copy = pltpu.make_async_remote_copy(
            src_ref=parts.at[to],
            dst_ref=got1.at[j - 1],
            send_sem=r1send.at[j - 1],
            recv_sem=r1recv.at[j - 1],
            device_id={"elem": group * n1 + to},
            device_id_type=MESH,
        )
        copy.start()
        copies.append(copy)
    for j in range(1, nband):
        for layer in range(2):
            for p in range(PIECES):
                field_copy(j, layer, p).wait_send()
    running = parts[member]
    for j, copy in enumerate(copies):
        copy.wait_recv()
        running += got1[j]
    mid[...] = running
    copies2 = []
    for j in range(1, n2):
        to = lax.rem(group + j, n2)
        copy = pltpu.make_async_remote_copy(
            src_ref=mid.at[to],
            dst_ref=got2.at[j - 1],
            send_sem=r2send.at[j - 1],
            recv_sem=r2recv.at[j - 1],
            device_id={"elem": to * n1 + member},
            device_id_type=MESH,
        )
        copy.start()
        copies2.append(copy)
    for copy in copies:
        copy.wait_send()
    final = mid[group]
    for j, copy in enumerate(copies2):
        copy.wait_recv()
        final += got2[j]
    for copy in copies2:
        copy.wait_send()
    written.wait()
    s_out[...] = final[0] * factor
    p_out[...] = final[1] * factor


def copy_kernel(field, s, p, f_out, s_out, p_out, sem):
    copy = pltpu.make_async_copy(field, f_out, sem)
    copy.start()
    s_out[...] = s[...]
    p_out[...] = p[...]
    copy.wait()


def body(n, nband, basis, hamiltonian, neighbours):
    bands, layers, cells, funcs = basis.shape
    total = layers * cells
    depth = layers * n
    rows = bands * nband // n
    n1 = 4
    n2 = n // n1
    nbr = neighbours.transpose(2, 0, 1)
    y0 = basis.reshape(bands, total, funcs).transpose(1, 2, 0)
    ham = hamiltonian.reshape(total * 7, funcs, funcs)
    factor = 1.0 / (depth * cells * funcs)
    geom = (n, nband, cells, n1, n2, rows, factor)
    vm = pl.BlockSpec(memory_space=pltpu.VMEM)
    half = (cells, funcs, bands)
    dma = pltpu.SemaphoreType.DMA
    small = jax.ShapeDtypeStruct((rows, bands), F32)
    field, s, p = pl.pallas_call(
        functools.partial(kernel, geom),
        out_shape=(jax.ShapeDtypeStruct((total, funcs, bands), BF16), small, small),
        in_specs=[
            pl.BlockSpec(memory_space=pltpu.SMEM),
            pl.BlockSpec(memory_space=pl.ANY),
            pl.BlockSpec(memory_space=pl.ANY),
        ],
        out_specs=(pl.BlockSpec(memory_space=pl.ANY), vm, vm),
        scratch_shapes=[
            pltpu.VMEM((total * 7, funcs, funcs), BF16),
            pltpu.VMEM((total, funcs, bands), BF16),
            pltpu.VMEM((total, funcs, bands), BF16),
            pltpu.VMEM((total, funcs, bands), BF16),
            pltpu.VMEM(half, BF16),
            pltpu.VMEM(half, BF16),
            pltpu.VMEM(half, BF16),
            pltpu.VMEM(half, BF16),
            pltpu.VMEM(half, BF16),
            pltpu.VMEM(half, BF16),
            pltpu.VMEM((total, funcs, bands), BF16),
            pltpu.VMEM((cells // PIECES, funcs, bands), F32),
            pltpu.VMEM((total, 2 * bands, funcs), BF16),
            pltpu.VMEM((nband, 2 * bands, bands), F32),
            pltpu.VMEM((nband - 1, 2, cells, funcs, bands), BF16),
            pltpu.VMEM((n1, n2, 2, rows, bands), F32),
            pltpu.VMEM((n1 - 1, n2, 2, rows, bands), F32),
            pltpu.VMEM((n2, 2, rows, bands), F32),
            pltpu.VMEM((n2 - 1, 2, rows, bands), F32),
            pltpu.SMEM((7, total), jnp.int32),
            dma((4,)),
            dma,
            dma,
            dma((DEGREE + 1,)),
            dma((DEGREE + 1,)),
            dma((DEGREE + 1, PIECES)),
            dma((DEGREE + 1, PIECES)),
            dma((nband - 1, 2, PIECES)),
            dma((nband - 1, 2, PIECES)),
            dma((n1 - 1,)),
            dma((n1 - 1,)),
            dma((n2 - 1,)),
            dma((n2 - 1,)),
        ],
        compiler_params=pltpu.CompilerParams(
            collective_id=0, has_side_effects=True, vmem_limit_bytes=56 * 1024 * 1024
        ),
    )(nbr, y0, ham)
    field, s, p = pl.pallas_call(
        copy_kernel,
        out_shape=(jax.ShapeDtypeStruct((total, funcs, bands), BF16), small, small),
        in_specs=[vm, vm, vm],
        out_specs=(pl.BlockSpec(memory_space=pl.ANY), vm, vm),
        scratch_shapes=[dma],
        compiler_params=pltpu.CompilerParams(vmem_limit_bytes=8 * 1024 * 1024),
    )(field, s, p)
    filtered = field.transpose(2, 0, 1).reshape(bands, layers, cells, funcs)
    return filtered, s, p


def solution(mesh):
    placed = (
        P("band", "elem", None, None),
        P("elem", None, None, None, None),
        P("elem", None, None),
    )
    return jax.shard_map(
        functools.partial(body, mesh.shape["elem"], mesh.shape["band"]),
        mesh=mesh,
        in_specs=placed,
        out_specs=(P("band", "elem", None, None), P("elem", "band"), P("elem", "band")),
        check_vma=False,
    )
```
